1024 devices in a mesh: row: 32 (over z), col: 32 (over x, y, core).
Axes of the slice: x: 4, y: 4, z: 32, core: 2. Of those that a mesh axis runs over, the one named last changes fastest.
Arguments:
- blocks: bfloat16 [2048, 8, 128, 128], P(('row', 'col')), may hold values from -1.5 to 1.5
- colidx: int32 [2048, 8], P(('row', 'col')), may hold values from 0 to 2047, as said below
- counts: int32 [32, 32], P('row', 'col'), may hold values from 1 to 66, as said below
- out_list: int32 [32, 32, 66], P('row', 'col'), may hold values from 0 to 65, as said below
Outputs:
- packed: bfloat16 [67584, 128, 128], P(('row', 'col'))
- offsets: int32 [32, 32], P('row', 'col')
The draws below stay inside these ranges and needn't reach their ends.
Inputs may be any that keep to these rules, and one draw needn't show every extreme that they name: `colidx`: block row i names 8 distinct block columns (i + e) mod 2048 with -8 <= e <= 8; among them are i, (i - 8) mod 2048 and (i + 8) mod 2048. `counts`: some device keeps all 66 blocks and some device keeps one. `out_list`: each device's list is an ordering of 0 to 65; only its first counts entries are used.
All inputs are finite; a program needn't handle non-finite values.
Results may differ from the reference program's by a relative error of at most 0.001.
Values may be sent and summed in bfloat16 or wider, within the bound.
No kernel may reach another device: no remote copies, remote signals or barrier semaphores. Data moves between devices by JAX's collectives and lax.ppermute only.
A program may use at most 64 MiB of HBM per device.

```python
import jax
import jax.numpy as jnp
from jax import lax

BS = 128
K = 8
H = 8
BR_DEV = 2
NB = 2048
TILE = 66
N_ROW = 32
N_COL = 32


def draw_colidx(key, part):
    pool_size = 2 * H - 2
    pool = jnp.concatenate([jnp.arange(1 - H, 0, dtype=jnp.int32), jnp.arange(1, H, dtype=jnp.int32)])
    scores = jax.random.randint(jax.random.fold_in(key, 5), (NB, pool_size), 0, 65536, dtype=jnp.int32)
    scores = scores * pool_size + jnp.arange(pool_size, dtype=jnp.int32)[None, :]
    order = jnp.argsort(scores, axis=-1)
    picked = jnp.take(pool, order[:, :K - 3])
    fixed = jnp.broadcast_to(jnp.array([-H, 0, H], dtype=jnp.int32)[None, :], (NB, 3))
    distances = jnp.sort(jnp.concatenate([fixed, picked], axis=1), axis=-1)
    block_rows = jnp.arange(NB, dtype=jnp.int32)[:, None]
    return ((block_rows + distances) % NB).astype(jnp.int32)


def draw_counts(key, part):
    key_values, key_high, key_low = jax.random.split(jax.random.fold_in(key, 7), 3)
    devices_all = N_ROW * N_COL
    values = jax.random.randint(key_values, (devices_all,), 1, TILE + 1, dtype=jnp.int32)
    high_spot = jax.random.randint(key_high, (), 0, devices_all, dtype=jnp.int32)
    low_spot = (high_spot + 1 + jax.random.randint(key_low, (), 0, devices_all - 1, dtype=jnp.int32)) % devices_all
    values = values.at[high_spot].set(TILE)
    values = values.at[low_spot].set(1)
    return values.reshape(N_ROW, N_COL).astype(jnp.int32)


def draw_out_list(key, part):
    scores = jax.random.randint(jax.random.fold_in(key, 11), (N_ROW, N_COL, TILE), 0, 65536, dtype=jnp.int32)
    scores = scores * TILE + jnp.arange(TILE, dtype=jnp.int32)[None, None, :]
    return jnp.argsort(scores, axis=-1).astype(jnp.int32)


def block_scale(rng, shape, cuts, low, top_value):
    loudness, own = 1.0, jax.random.fold_in(rng, 6)
    for position, shards_of in cuts:
        draws = jnp.exp(jax.random.uniform(jax.random.fold_in(own, position), (shards_of,), jnp.float32, low / len(cuts), top_value / len(cuts)))
        loudness = loudness * jnp.repeat(draws, shape[position] // shards_of).reshape([-1 if axis == position else 1 for axis in range(len(shape))])
    return loudness


def bell_draw(rng, shape, spread, bound, shards=(), kind=jnp.bfloat16):
    values = jax.random.normal(rng, shape, jnp.float32) * spread
    if len(shards) > 0:
        values = block_scale(rng, shape, shards, -0.22, 0.18) * values
    return jnp.clip(values, min=-bound, max=bound).astype(kind)


def setup_inputs(seed: int = 0) -> dict:
    keys = jax.random.split(jax.random.key(seed), 5)
    blocks = bell_draw(keys[0], (NB, K, BS, BS), 0.25, 1.5, ((0, 1024),))
    colidx = draw_colidx(jax.random.fold_in(keys[4], 71), 0)
    counts = draw_counts(jax.random.fold_in(keys[4], 71), 0)
    out_list = draw_out_list(jax.random.fold_in(keys[4], 71), 0)
    return {"blocks": blocks, "colidx": colidx, "counts": counts, "out_list": out_list}


def device_packed(blocks, colidx, counts, out_list, device):
    grid_row = device // N_COL
    grid_col = device % N_COL
    first_row = device * BR_DEV
    band_size = 4 * H + 1

    def row_band(local_row):
        block_row = (first_row + local_row).astype(jnp.int32)
        a_blocks = lax.dynamic_index_in_dim(blocks, block_row, 0, keepdims=False)
        a_cols = lax.dynamic_index_in_dim(colidx, block_row, 0, keepdims=False)
        b_blocks = jnp.take(blocks, a_cols, axis=0)
        b_cols = jnp.take(colidx, a_cols, axis=0)
        products = jnp.einsum("tab,tubc->tuac", a_blocks.astype(jnp.float32), b_blocks.astype(jnp.float32),
                              precision=lax.Precision.HIGHEST)
        places = ((b_cols - block_row + 2 * H) % NB).astype(jnp.int32)
        onehot = (places[:, :, None] == jnp.arange(band_size, dtype=jnp.int32)[None, None, :]).astype(jnp.float32)
        return jnp.einsum("tuf,tuac->fac", onehot, products, precision=lax.Precision.HIGHEST)

    grid_tile = lax.map(row_band, jnp.arange(BR_DEV, dtype=jnp.int32))
    flattened = grid_tile.reshape(TILE, BS, BS)
    listing = out_list[grid_row, grid_col]
    picked = jnp.take(flattened, listing, axis=0)
    in_list = jnp.arange(TILE, dtype=jnp.int32) < counts[grid_row, grid_col]
    return jnp.where(in_list[:, None, None], picked, jnp.zeros_like(picked)).astype(jnp.bfloat16)


def reference(blocks, colidx, counts, out_list):
    indices = jnp.arange(N_ROW * N_COL, dtype=jnp.int32)
    stacked = lax.map(lambda device: device_packed(blocks, colidx, counts, out_list, device), indices)
    packed = stacked.reshape(N_ROW * N_COL * TILE, BS, BS)
    flat_counts = counts.reshape(-1)
    offsets = (jnp.cumsum(flat_counts) - flat_counts).astype(jnp.int32).reshape(N_ROW, N_COL)
    return packed, offsets
```

```python
import jax
import jax.numpy as jnp
from jax import lax
from jax.experimental import pallas as pl
from jax.experimental.pallas import tpu as pltpu
from jax.sharding import Mesh, PartitionSpec as P


H = 8
LANES = 128
META_ROWS = 16
ALL = ("row", "x", "y", "core")

OWN, I0, S1, S2, I1, I2, F1, I3, F2 = range(9)
SIDE_STEPS = {OWN: 0, I0: 1, S1: 2, S2: -2, I1: -1, I2: 3, F1: 4, I3: -3, F2: -4}


def chip_pairs(devices, step):
    return [(d, (d + 2 * (step if d % 2 == 0 else -step)) % devices) for d in range(devices)]


def core_pairs(devices):
    return [(d, d ^ 1) for d in range(devices)]


def far_pairs(rows, cols):
    return [(r * cols + c, (r + c) % rows * cols + c) for r in range(rows) for c in range(1, cols)]


def product_kernel(params, *refs):
    pieces = refs[:9]
    out = refs[9]
    near, acc, meta_vec, stage, meta, slot, load_sems, meta_sem, out_sems = refs[10:]
    tiles = acc.shape[0]
    band = tiles // 2
    size = acc.shape[1]
    slots = near.shape[1] // size // 2
    side = params[0]
    count = params[1]
    loads = []
    for p in range(9):
        copy = pltpu.make_async_copy(pieces[p], near.at[p], load_sems.at[p])
        copy.start()
        loads.append(copy)
    acc[...] = jnp.zeros_like(acc)

    @pl.loop(0, 2 * (2 * H + 2))
    def _(k):
        slot[k] = -1

    @pl.loop(0, 2 * slots)
    def _(k):
        a = k // slots
        slot[a * (2 * H + 2) + params[2 + k] + H + a] = k - a * slots

    first = 2 * slots * size
    for p in range(9):
        loads[p].wait()
        meta_vec[p:p + 1, :] = near[p, first:first + META_ROWS, :].astype(jnp.float32)[0:1, :].astype(jnp.int32)
    to_smem = pltpu.make_async_copy(meta_vec, meta, meta_sem)
    to_smem.start()
    to_smem.wait()
    for p in range(9):
        base = 2 * (SIDE_STEPS[p] * side + H // 2)

        @pl.loop(0, 4)
        def _(j):
            b = j // 2
            a = j - 2 * b
            rel = base + b
            t = slot[a * (2 * H + 2) + rel]

            @pl.when(t >= 0)
            def _():
                a_block = near[OWN, pl.ds(pl.multiple_of((a * slots + t) * size, size), size), :]
                shift = a * band + rel + H - a
                for u in range(0, slots, 2):
                    start = pl.multiple_of((b * slots + u) * size, size)
                    pair = jnp.concatenate(
                        [near[p, pl.ds(start, size), :], near[p, pl.ds(start + size, size), :]], axis=1
                    )
                    both = jnp.dot(a_block, pair, preferred_element_type=jnp.float32)
                    f = shift + meta[p, b * slots + u]
                    acc[f] = acc[f] + both[:, :size]
                    g = shift + meta[p, b * slots + u + 1]
                    acc[g] = acc[g] + both[:, size:]

    chunks = out_sems.shape[0]
    per = tiles // chunks
    stores = []
    for c in range(chunks):

        @pl.loop(c * per, (c + 1) * per)
        def _(p):
            @pl.when(p < count)
            def _():
                stage[p] = acc[params[2 + 2 * slots + p]].astype(stage.dtype)

            @pl.when(p >= count)
            def _():
                stage[p] = jnp.zeros((size, size), stage.dtype)

        copy = pltpu.make_async_copy(stage.at[pl.ds(c * per, per)], out.at[pl.ds(c * per, per)], out_sems.at[c])
        copy.start()
        stores.append(copy)
    for copy in stores:
        copy.wait()


def products(params, pieces, tiles, size):
    rows = pieces[0].shape[0]
    chunks = 6
    return pl.pallas_call(
        product_kernel,
        out_shape=jax.ShapeDtypeStruct((tiles, size, size), jnp.bfloat16),
        in_specs=[pl.BlockSpec(memory_space=pltpu.SMEM)] + [pl.BlockSpec(memory_space=pl.ANY)] * 9,
        out_specs=pl.BlockSpec(memory_space=pl.ANY),
        scratch_shapes=[
            pltpu.VMEM((9, rows, LANES), jnp.bfloat16),
            pltpu.VMEM((tiles, size, size), jnp.float32),
            pltpu.VMEM((16, LANES), jnp.int32),
            pltpu.VMEM((tiles, size, size), jnp.bfloat16),
            pltpu.SMEM((16, LANES), jnp.int32),
            pltpu.SMEM((64,), jnp.int32),
            pltpu.SemaphoreType.DMA((9,)),
            pltpu.SemaphoreType.DMA,
            pltpu.SemaphoreType.DMA((chunks,)),
        ],
        compiler_params=pltpu.CompilerParams(vmem_limit_bytes=24 * 1024 * 1024),
        cost_estimate=pl.CostEstimate(flops=600_000_000, bytes_accessed=8_000_000, transcendentals=0),
        name="products",
    )(params, *pieces)


def make_shards(shape):
    rows_of = shape["row"]
    cols_of = shape["x"] * shape["y"] * shape["core"]
    devices = rows_of * cols_of

    def compute(blocks, colidx, counts, out_list):
        here, slots, size = blocks.shape[:3]
        grid_row = lax.axis_index("row")
        col = lax.axis_index(("x", "y", "core"))
        device = grid_row * cols_of + col
        total = here * devices
        row_ids = device * here + jnp.arange(here, dtype=jnp.int32)[:, None]
        away = (colidx - row_ids + H) % total - H
        meta = jnp.zeros((META_ROWS, LANES), jnp.bfloat16).at[:, : here * slots].set(
            away.reshape(1, -1).astype(jnp.bfloat16)
        )
        own = jnp.concatenate([blocks.reshape(here * slots * size, size), meta], axis=0)

        def send(x, pairs):
            return lax.ppermute(x, ALL, pairs)

        down, up, swap = chip_pairs(devices, -1), chip_pairs(devices, 1), core_pairs(devices)
        s1 = send(own, down)
        s2 = send(own, up)
        f1 = send(s1, down)
        f2 = send(s2, up)
        i0 = send(own, swap)
        i1 = send(s1, swap)
        i2 = send(s2, swap)
        i3 = send(f1, swap)

        lane = jnp.arange(LANES, dtype=jnp.int32)
        kept = counts[0, 0]
        row_counts = jnp.where(lane == col, kept, 0)
        row_counts = lax.psum(row_counts, ("y", "core"))
        row_counts = lax.psum(row_counts, "x")
        within = jnp.sum(jnp.where(lane < col, row_counts, 0))
        row_total = jnp.broadcast_to(jnp.sum(row_counts), (LANES,))
        far = send(row_total, far_pairs(rows_of, cols_of))
        far, _ = lax.optimization_barrier((far, f1))
        before = jnp.where((col >= 1) & (col <= grid_row), far, 0)
        before = lax.psum(before, ("y", "core"))
        before = lax.psum(before, "x")
        offsets = (before[0] + within).astype(jnp.int32).reshape(1, 1)

        side = 1 - 2 * (col % 2)
        tiles = here * (4 * H + 1)
        params = jnp.concatenate(
            [side.reshape(1), counts.reshape(1), away.reshape(-1), out_list.reshape(-1)]
        ).astype(jnp.int32)
        by_name = {OWN: own, I0: i0, S1: s1, S2: s2, I1: i1, I2: i2, F1: f1, I3: i3, F2: f2}
        packed = products(params, [by_name[p] for p in range(9)], tiles, size)
        return (packed, offsets)

    return compute


def solution(mesh):
    rows_of, cols_of = mesh.shape["row"], mesh.shape["col"]
    fine = Mesh(mesh.devices.reshape(rows_of, cols_of // 8, 4, 2), ALL)
    col = ("x", "y", "core")
    in_specs = (
        P(ALL, None, None, None),
        P(ALL, None),
        P("row", col),
        P("row", col, None),
    )
    out_specs = (P(ALL, None, None), P("row", col))
    return jax.shard_map(
        make_shards(dict(fine.shape)), mesh=fine, in_specs=in_specs, out_specs=out_specs, check_vma=False
    )
```

```python
import functools

import jax
import jax.numpy as jnp
from jax import lax
from jax.experimental import pallas as pl
from jax.experimental.pallas import tpu as pltpu
from jax.sharding import Mesh, PartitionSpec as P


H = 8
LANES = 128
META_ROWS = 16
VMEM_GRANT = 58 * 1024 * 1024
ALL = ("row", "x", "y", "core")

OWN, I0, S1, S2, I1, I2, F1, I3, F2 = range(9)
SIDE_STEPS = {OWN: 0, I0: 1, S1: 2, S2: -2, I1: -1, I2: 3, F1: 4, I3: -3, F2: -4}


def chip_pairs(devices, step):
    return [(d, (d + 2 * (step if d % 2 == 0 else -step)) % devices) for d in range(devices)]


def core_pairs(devices):
    return [(d, d ^ 1) for d in range(devices)]


def far_pairs(rows, cols):
    return [(r * cols + c, (r + c) % rows * cols + c) for r in range(rows) for c in range(1, cols)]


def build_slots(params, slot, slots):
    reach = 2 * H + 2

    @pl.loop(0, 2 * reach)
    def _(k):
        slot[k] = -1

    @pl.loop(0, 2 * slots)
    def _(k):
        a = k // slots
        slot[a * reach + params[2 + k] + H + a] = k - a * slots


def add_products(p, kind, side, own, piece, acc, slot, meta, slots):
    size = acc.shape[1]
    band = acc.shape[0] // 2
    base = 2 * (SIDE_STEPS[kind] * side + H // 2)

    @pl.loop(0, 4)
    def _(j):
        b = j // 2
        a = j - 2 * b
        rel = base + b
        t = slot[a * (2 * H + 2) + rel]

        @pl.when(t >= 0)
        def _():
            a_block = own[pl.ds(pl.multiple_of((a * slots + t) * size, size), size), :]
            shift = a * band + rel + H - a
            for u in range(0, slots, 2):
                start = pl.multiple_of((b * slots + u) * size, size)
                pair = jnp.concatenate(
                    [piece[pl.ds(start, size), :], piece[pl.ds(start + size, size), :]], axis=1
                )
                both = jnp.dot(a_block, pair, preferred_element_type=jnp.float32)
                f = shift + meta[2 * p + b, u]
                acc[f] = acc[f] + both[:, :size]
                g = shift + meta[2 * p + b, u + 1]
                acc[g] = acc[g] + both[:, size:]


def load_pieces(pieces, near, meta_raw, load_sems, meta_sems):
    metas = []
    loads = []
    for p, piece in enumerate(pieces):
        rows = piece.shape[0] - META_ROWS
        copy = pltpu.make_async_copy(piece.at[pl.ds(rows, META_ROWS)], meta_raw.at[p], meta_sems.at[p])
        copy.start()
        metas.append(copy)
    for p, piece in enumerate(pieces):
        rows = piece.shape[0] - META_ROWS
        copy = pltpu.make_async_copy(piece.at[pl.ds(0, rows)], near.at[p], load_sems.at[p])
        copy.start()
        loads.append(copy)
    return metas, loads


def read_meta(metas, meta_raw, meta_vec, meta, sem):
    for p, copy in enumerate(metas):
        copy.wait()
        meta_vec[2 * p:2 * p + 2, :] = meta_raw[p].astype(jnp.float32)[0:2, :].astype(jnp.int32)
    copy = pltpu.make_async_copy(meta_vec, meta, sem)
    copy.start()
    return copy


def early_kernel(kinds, slots, params, *refs):
    n = len(kinds)
    pieces = refs[:n]
    acc_out, near, acc, meta_raw, meta_vec, meta, slot, load_sems, meta_sems, sem, acc_sem = refs[n:]
    metas, loads = load_pieces(pieces, near, meta_raw, load_sems, meta_sems)
    copy = read_meta(metas, meta_raw, meta_vec, meta, sem)
    build_slots(params, slot, slots)
    acc[...] = jnp.zeros_like(acc)
    copy.wait()
    for p, kind in enumerate(kinds):
        loads[p].wait()
        add_products(p, kind, params[0], near.at[0], near.at[p], acc, slot, meta, slots)
    save = pltpu.make_async_copy(acc, acc_out, acc_sem)
    save.start()
    save.wait()


def late_kernel(kinds, slots, params, own, acc_in, *refs):
    n = len(kinds)
    pieces = refs[:n]
    out, a_rows, near, acc, meta_raw, meta_vec, stage, meta, slot = refs[n:n + 9]
    load_sems, meta_sems, sem, own_sem, acc_sem, out_sems = refs[n + 9:]
    tiles, size = acc.shape[:2]
    own_load = pltpu.make_async_copy(own.at[pl.ds(0, 2 * slots * size)], a_rows, own_sem)
    own_load.start()
    load = pltpu.make_async_copy(acc_in, acc, acc_sem)
    load.start()
    metas, loads = load_pieces(pieces, near, meta_raw, load_sems, meta_sems)
    copy = read_meta(metas, meta_raw, meta_vec, meta, sem)
    build_slots(params, slot, slots)
    copy.wait()
    own_load.wait()
    load.wait()
    for p, kind in enumerate(kinds):
        loads[p].wait()
        add_products(p, kind, params[0], a_rows, near.at[p], acc, slot, meta, slots)
    count = params[1]
    chunks = out_sems.shape[0]
    per = tiles // chunks
    stores = []
    for c in range(chunks):

        @pl.loop(c * per, (c + 1) * per)
        def _(p):
            @pl.when(p < count)
            def _():
                stage[p] = acc[params[2 + 2 * slots + p]].astype(stage.dtype)

            @pl.when(p >= count)
            def _():
                stage[p] = jnp.zeros((size, size), stage.dtype)

        copy = pltpu.make_async_copy(stage.at[pl.ds(c * per, per)], out.at[pl.ds(c * per, per)], out_sems.at[c])
        copy.start()
        stores.append(copy)
    for copy in stores:
        copy.wait()


def scratch(n, tiles, size, slots):
    return [
        pltpu.VMEM((n, 2 * slots * size, size), jnp.bfloat16),
        pltpu.VMEM((tiles, size, size), jnp.float32),
        pltpu.VMEM((n, META_ROWS, LANES), jnp.bfloat16),
        pltpu.VMEM((16, LANES), jnp.int32),
    ]


def early_products(params, kinds, pieces, tiles, size, slots):
    n = len(kinds)
    return pl.pallas_call(
        functools.partial(early_kernel, kinds, slots),
        out_shape=jax.ShapeDtypeStruct((tiles, size, size), jnp.float32),
        in_specs=[pl.BlockSpec(memory_space=pltpu.SMEM)] + [pl.BlockSpec(memory_space=pl.ANY)] * n,
        out_specs=pl.BlockSpec(memory_space=pl.ANY),
        scratch_shapes=scratch(n, tiles, size, slots)
        + [
            pltpu.SMEM((16, LANES), jnp.int32),
            pltpu.SMEM((64,), jnp.int32),
            pltpu.SemaphoreType.DMA((n,)),
            pltpu.SemaphoreType.DMA((n,)),
            pltpu.SemaphoreType.DMA,
            pltpu.SemaphoreType.DMA,
        ],
        compiler_params=pltpu.CompilerParams(vmem_limit_bytes=VMEM_GRANT),
        cost_estimate=pl.CostEstimate(flops=300_000_000, bytes_accessed=4_000_000, transcendentals=0),
        name="early",
    )(params, *pieces)


def late_products(params, own, acc, kinds, pieces, slots):
    tiles, size = acc.shape[:2]
    n = len(kinds)
    chunks = 6
    return pl.pallas_call(
        functools.partial(late_kernel, kinds, slots),
        out_shape=jax.ShapeDtypeStruct((tiles, size, size), jnp.bfloat16),
        in_specs=[pl.BlockSpec(memory_space=pltpu.SMEM)] + [pl.BlockSpec(memory_space=pl.ANY)] * (n + 2),
        out_specs=pl.BlockSpec(memory_space=pl.ANY),
        scratch_shapes=[pltpu.VMEM((2 * slots * size, size), jnp.bfloat16)]
        + scratch(n, tiles, size, slots)
        + [
            pltpu.VMEM((tiles, size, size), jnp.bfloat16),
            pltpu.SMEM((16, LANES), jnp.int32),
            pltpu.SMEM((64,), jnp.int32),
            pltpu.SemaphoreType.DMA((n,)),
            pltpu.SemaphoreType.DMA((n,)),
            pltpu.SemaphoreType.DMA,
            pltpu.SemaphoreType.DMA,
            pltpu.SemaphoreType.DMA,
            pltpu.SemaphoreType.DMA((chunks,)),
        ],
        compiler_params=pltpu.CompilerParams(vmem_limit_bytes=VMEM_GRANT),
        cost_estimate=pl.CostEstimate(flops=300_000_000, bytes_accessed=6_000_000, transcendentals=0),
        name="late",
    )(params, own, acc, *pieces)


def make_shards(shape):
    rows_of = shape["row"]
    cols_of = shape["x"] * shape["y"] * shape["core"]
    devices = rows_of * cols_of

    def compute(blocks, colidx, counts, out_list):
        here, slots, size = blocks.shape[:3]
        grid_row = lax.axis_index("row")
        col = lax.axis_index(("x", "y", "core"))
        device = grid_row * cols_of + col
        total = here * devices
        row_ids = device * here + jnp.arange(here, dtype=jnp.int32)[:, None]
        away = colidx - row_ids
        away = jnp.where(away > H, away - total, jnp.where(away < -H, away + total, away))
        meta = jnp.pad(away.astype(jnp.bfloat16), ((0, META_ROWS - here), (0, LANES - slots)))
        own = jnp.concatenate([blocks.reshape(here * slots * size, size), meta], axis=0)

        def send(x, pairs):
            return lax.ppermute(x, ALL, pairs)

        down, up, swap = chip_pairs(devices, -1), chip_pairs(devices, 1), core_pairs(devices)
        s1 = send(own, down)
        s2 = send(own, up)
        f1 = send(s1, down)
        f2 = send(s2, up)
        i0 = send(own, swap)
        i1 = send(s1, swap)
        i2 = send(s2, swap)
        i3 = send(f1, swap)

        lane = jnp.arange(LANES, dtype=jnp.int32)
        kept = counts[0, 0]
        row_counts = jnp.where(lane == col, kept, 0)
        row_counts = lax.psum(row_counts, "x")
        row_counts = lax.psum(row_counts, ("y", "core"))
        within = jnp.sum(jnp.where(lane < col, row_counts, 0))
        row_total = jnp.broadcast_to(jnp.sum(row_counts), (LANES,))
        far = send(row_total, far_pairs(rows_of, cols_of))
        before = jnp.where((col >= 1) & (col <= grid_row), far, 0)
        before = lax.psum(before, "x")
        before = lax.psum(before, ("y", "core"))
        offsets = (before[0] + within).astype(jnp.int32).reshape(1, 1)

        side = 1 - 2 * (col % 2)
        tiles = here * (4 * H + 1)
        params = jnp.concatenate(
            [side.reshape(1), counts.reshape(1), away.reshape(-1), out_list.reshape(-1)]
        ).astype(jnp.int32)
        acc = early_products(params, (OWN, I0, S1, I1), (own, i0, s1, i1), tiles, size, slots)
        packed = late_products(params, own, acc, (S2, I2, F1, I3, F2), (s2, i2, f1, i3, f2), slots)
        return (packed, offsets)

    return compute


def solution(mesh):
    rows_of, cols_of = mesh.shape["row"], mesh.shape["col"]
    fine = Mesh(mesh.devices.reshape(rows_of, cols_of // 8, 4, 2), ALL)
    col = ("x", "y", "core")
    in_specs = (
        P(ALL, None, None, None),
        P(ALL, None),
        P("row", col),
        P("row", col, None),
    )
    out_specs = (P(ALL, None, None), P("row", col))
    return jax.shard_map(
        make_shards(dict(fine.shape)), mesh=fine, in_specs=in_specs, out_specs=out_specs, check_vma=False
    )
```

```python
import functools

import jax
import jax.numpy as jnp
from jax import lax
from jax.experimental import pallas as pl
from jax.experimental.pallas import tpu as pltpu
from jax.sharding import Mesh, PartitionSpec as P


H = 8
LANES = 128
COPIES = 4
META_ROWS = 16
ALL = ("row", "x", "y", "core")

OWN, I0, S1, S2, I1, I2, F1, I3, F2 = range(9)
SIDE_STEPS = {OWN: 0, I0: 1, S1: 2, S2: -2, I1: -1, I2: 3, F1: 4, I3: -3, F2: -4}


def chip_pairs(devices, step):
    return [(d, (d + 2 * (step if d % 2 == 0 else -step)) % devices) for d in range(devices)]


def core_pairs(devices):
    return [(d, d ^ 1) for d in range(devices)]


def product_kernel(slots, params, *refs):
    pieces = refs[:9]
    out, near, acc, meta_raw, meta_vec, stage, meta, load_sems, meta_sems, meta_sem, out_sems = refs[9:]
    tiles, size = acc.shape[:2]
    band = tiles // 2
    rows = 2 * slots * size
    reach = 2 * H + 2
    side = params[0]
    count = params[1]
    metas = []
    loads = []
    for p in range(9):
        copy = pltpu.make_async_copy(pieces[p].at[pl.ds(rows, META_ROWS)], meta_raw.at[p], meta_sems.at[p])
        copy.start()
        metas.append(copy)
    for p in range(9):
        copy = pltpu.make_async_copy(pieces[p].at[pl.ds(0, rows)], near.at[p], load_sems.at[p])
        copy.start()
        loads.append(copy)
    for p in range(9):
        metas[p].wait()
        meta_vec[2 * p:2 * p + 2, :] = meta_raw[p].astype(jnp.float32)[0:2, :].astype(jnp.int32)
    to_smem = pltpu.make_async_copy(meta_vec, meta, meta_sem)
    to_smem.start()
    acc[...] = jnp.zeros_like(acc)
    to_smem.wait()
    for p in range(9):
        loads[p].wait()
        base = 2 * (SIDE_STEPS[p] * side + H // 2)

        @pl.loop(0, 4)
        def _(j):
            b = j // 2
            a = j - 2 * b
            rel = base + b
            t = params[2 + a * reach + rel]

            @pl.when(t >= 0)
            def _():
                a_block = near[OWN, pl.ds(pl.multiple_of((a * slots + t) * size, size), size), :]
                shift = a * band + rel + H - a
                for u in range(0, slots, 2):
                    start = pl.multiple_of((b * slots + u) * size, size)
                    pair = jnp.concatenate(
                        [near[p, pl.ds(start, size), :], near[p, pl.ds(start + size, size), :]], axis=1
                    )
                    both = jnp.dot(a_block, pair, preferred_element_type=jnp.float32)
                    f = shift + meta[2 * p + b, u]
                    acc[f] = acc[f] + both[:, :size]
                    g = shift + meta[2 * p + b, u + 1]
                    acc[g] = acc[g] + both[:, size:]

    chunks = out_sems.shape[0]
    per = tiles // chunks
    stores = []
    for c in range(chunks):

        @pl.loop(c * per, (c + 1) * per)
        def _(p):
            @pl.when(p < count)
            def _():
                stage[p] = acc[params[2 + 2 * reach + p]].astype(stage.dtype)

            @pl.when(p >= count)
            def _():
                stage[p] = jnp.zeros((size, size), stage.dtype)

        copy = pltpu.make_async_copy(stage.at[pl.ds(c * per, per)], out.at[pl.ds(c * per, per)], out_sems.at[c])
        copy.start()
        stores.append(copy)
    for copy in stores:
        copy.wait()


def products(params, pieces, tiles, size, slots):
    chunks = 6
    return pl.pallas_call(
        functools.partial(product_kernel, slots),
        out_shape=jax.ShapeDtypeStruct((tiles, size, size), jnp.bfloat16),
        in_specs=[pl.BlockSpec(memory_space=pltpu.SMEM)] + [pl.BlockSpec(memory_space=pl.ANY)] * 9,
        out_specs=pl.BlockSpec(memory_space=pl.ANY),
        scratch_shapes=[
            pltpu.VMEM((9, 2 * slots * size, LANES), jnp.bfloat16),
            pltpu.VMEM((tiles, size, size), jnp.float32),
            pltpu.VMEM((9, META_ROWS, LANES), jnp.bfloat16),
            pltpu.VMEM((24, LANES), jnp.int32),
            pltpu.VMEM((tiles, size, size), jnp.bfloat16),
            pltpu.SMEM((24, LANES), jnp.int32),
            pltpu.SemaphoreType.DMA((9,)),
            pltpu.SemaphoreType.DMA((9,)),
            pltpu.SemaphoreType.DMA,
            pltpu.SemaphoreType.DMA((chunks,)),
        ],
        compiler_params=pltpu.CompilerParams(vmem_limit_bytes=24 * 1024 * 1024),
        cost_estimate=pl.CostEstimate(flops=600_000_000, bytes_accessed=8_000_000, transcendentals=0),
        name="products",
    )(params, *pieces)


def make_shards(shape):
    rows_of = shape["row"]
    cols_of = shape["x"] * shape["y"] * shape["core"]
    devices = rows_of * cols_of

    def compute(blocks, colidx, counts, out_list):
        here, slots, size = blocks.shape[:3]
        grid_row = lax.axis_index("row")
        col = lax.axis_index(("x", "y", "core"))
        device = grid_row * cols_of + col
        total = here * devices
        row_ids = device * here + jnp.arange(here, dtype=jnp.int32)[:, None]
        away = colidx - row_ids
        away = jnp.where(away > H, away - total, jnp.where(away < -H, away + total, away))
        meta = jnp.pad(away.astype(jnp.bfloat16), ((0, META_ROWS - here), (0, LANES - slots)))
        own = jnp.concatenate([blocks.reshape(here * slots * size, size), meta], axis=0)

        def send(x, pairs):
            return lax.ppermute(x, ALL, pairs)

        down, up, swap = chip_pairs(devices, -1), chip_pairs(devices, 1), core_pairs(devices)
        s1 = send(own, down)
        s2 = send(own, up)
        f1 = send(s1, down)
        f2 = send(s2, up)
        i0 = send(own, swap)
        i1 = send(s1, swap)
        i2 = send(s2, swap)
        i3 = send(f1, swap)

        mine = lax.optimization_barrier(jnp.broadcast_to(counts, (COPIES, LANES)))
        all_counts = lax.optimization_barrier(lax.all_gather(mine, ALL, axis=0, tiled=True))
        first = all_counts.reshape(devices, COPIES, LANES)[:, 0, :]
        earlier = jnp.arange(devices, dtype=jnp.int32)[:, None] < device
        offsets = jnp.sum(jnp.where(earlier, first, 0), axis=0)[:1].astype(jnp.int32).reshape(1, 1)

        side = 1 - 2 * (col % 2)
        tiles = here * (4 * H + 1)
        reach = jnp.arange(2 * H + 2, dtype=jnp.int32)
        spot = away + H + jnp.arange(here, dtype=jnp.int32)[:, None]
        hit = spot[:, :, None] == reach[None, None, :]
        slot = jnp.sum(jnp.where(hit, jnp.arange(1, slots + 1, dtype=jnp.int32)[None, :, None], 0), axis=1) - 1
        params = jnp.concatenate(
            [side.reshape(1), counts.reshape(1), slot.reshape(-1), out_list.reshape(-1)]
        ).astype(jnp.int32)
        by_name = {OWN: own, I0: i0, S1: s1, S2: s2, I1: i1, I2: i2, F1: f1, I3: i3, F2: f2}
        packed = products(params, [by_name[p] for p in range(9)], tiles, size, slots)
        return (packed, offsets)

    return compute


def solution(mesh):
    rows_of, cols_of = mesh.shape["row"], mesh.shape["col"]
    fine = Mesh(mesh.devices.reshape(rows_of, cols_of // 8, 4, 2), ALL)
    col = ("x", "y", "core")
    in_specs = (
        P(ALL, None, None, None),
        P(ALL, None),
        P("row", col),
        P("row", col, None),
    )
    out_specs = (P(ALL, None, None), P("row", col))
    return jax.shard_map(
        make_shards(dict(fine.shape)), mesh=fine, in_specs=in_specs, out_specs=out_specs, check_vma=False
    )
```

```python
import functools

import jax
import jax.numpy as jnp
from jax import lax
from jax.experimental import pallas as pl
from jax.experimental.pallas import tpu as pltpu
from jax.sharding import Mesh, PartitionSpec as P


H = 8
LANES = 128
META_ROWS = 16
ALL = ("row", "x", "y", "core")

OWN, I0, S1, S2, I1, I2, F1, I3, F2 = range(9)
SIDE_STEPS = {OWN: 0, I0: 1, S1: 2, S2: -2, I1: -1, I2: 3, F1: 4, I3: -3, F2: -4}


def chip_pairs(devices, step):
    return [(d, (d + 2 * (step if d % 2 == 0 else -step)) % devices) for d in range(devices)]


def core_pairs(devices):
    return [(d, d ^ 1) for d in range(devices)]


def far_pairs(rows, cols):
    return [(r * cols + c, (r + c) % rows * cols + c) for r in range(rows) for c in range(1, cols)]


def product_kernel(slots, params, *refs):
    pieces = refs[:9]
    out, near, acc, meta_raw, meta_vec, stage, meta, load_sems, meta_sems, meta_sem, out_sems = refs[9:]
    tiles, size = acc.shape[:2]
    band = tiles // 2
    rows = 2 * slots * size
    reach = 2 * H + 2
    side = params[0]
    count = params[1]
    metas = []
    loads = []
    for p in range(9):
        copy = pltpu.make_async_copy(pieces[p].at[pl.ds(rows, META_ROWS)], meta_raw.at[p], meta_sems.at[p])
        copy.start()
        metas.append(copy)
    for p in range(9):
        copy = pltpu.make_async_copy(pieces[p].at[pl.ds(0, rows)], near.at[p], load_sems.at[p])
        copy.start()
        loads.append(copy)
    acc[...] = jnp.zeros_like(acc)
    for p in range(9):
        metas[p].wait()
        meta_vec[2 * p:2 * p + 2, :] = meta_raw[p].astype(jnp.float32)[0:2, :].astype(jnp.int32)
    to_smem = pltpu.make_async_copy(meta_vec, meta, meta_sem)
    to_smem.start()
    to_smem.wait()
    for p in range(9):
        loads[p].wait()
        base = 2 * (SIDE_STEPS[p] * side + H // 2)

        @pl.loop(0, 4)
        def _(j):
            b = j // 2
            a = j - 2 * b
            rel = base + b
            t = params[2 + a * reach + rel]

            @pl.when(t >= 0)
            def _():
                a_block = near[OWN, pl.ds(pl.multiple_of((a * slots + t) * size, size), size), :]
                shift = a * band + rel + H - a
                for u in range(0, slots, 2):
                    start = pl.multiple_of((b * slots + u) * size, size)
                    pair = jnp.concatenate(
                        [near[p, pl.ds(start, size), :], near[p, pl.ds(start + size, size), :]], axis=1
                    )
                    both = jnp.dot(a_block, pair, preferred_element_type=jnp.float32)
                    f = shift + meta[2 * p + b, u]
                    acc[f] = acc[f] + both[:, :size]
                    g = shift + meta[2 * p + b, u + 1]
                    acc[g] = acc[g] + both[:, size:]

    chunks = out_sems.shape[0]
    per = tiles // chunks
    stores = []
    for c in range(chunks):

        @pl.loop(c * per, (c + 1) * per)
        def _(p):
            @pl.when(p < count)
            def _():
                stage[p] = acc[params[2 + 2 * reach + p]].astype(stage.dtype)

            @pl.when(p >= count)
            def _():
                stage[p] = jnp.zeros((size, size), stage.dtype)

        copy = pltpu.make_async_copy(stage.at[pl.ds(c * per, per)], out.at[pl.ds(c * per, per)], out_sems.at[c])
        copy.start()
        stores.append(copy)
    for copy in stores:
        copy.wait()


def products(params, pieces, tiles, size, slots):
    chunks = 6
    return pl.pallas_call(
        functools.partial(product_kernel, slots),
        out_shape=jax.ShapeDtypeStruct((tiles, size, size), jnp.bfloat16),
        in_specs=[pl.BlockSpec(memory_space=pltpu.SMEM)] + [pl.BlockSpec(memory_space=pl.ANY)] * 9,
        out_specs=pl.BlockSpec(memory_space=pl.ANY),
        scratch_shapes=[
            pltpu.VMEM((9, 2 * slots * size, LANES), jnp.bfloat16),
            pltpu.VMEM((tiles, size, size), jnp.float32),
            pltpu.VMEM((9, META_ROWS, LANES), jnp.bfloat16),
            pltpu.VMEM((24, LANES), jnp.int32),
            pltpu.VMEM((tiles, size, size), jnp.bfloat16),
            pltpu.SMEM((24, LANES), jnp.int32),
            pltpu.SemaphoreType.DMA((9,)),
            pltpu.SemaphoreType.DMA((9,)),
            pltpu.SemaphoreType.DMA,
            pltpu.SemaphoreType.DMA((chunks,)),
        ],
        compiler_params=pltpu.CompilerParams(vmem_limit_bytes=24 * 1024 * 1024),
        cost_estimate=pl.CostEstimate(flops=600_000_000, bytes_accessed=8_000_000, transcendentals=0),
        name="products",
    )(params, *pieces)


def make_shards(shape):
    rows_of = shape["row"]
    cols_of = shape["x"] * shape["y"] * shape["core"]
    devices = rows_of * cols_of

    def compute(blocks, colidx, counts, out_list):
        here, slots, size = blocks.shape[:3]
        grid_row = lax.axis_index("row")
        col = lax.axis_index(("x", "y", "core"))
        device = grid_row * cols_of + col
        total = here * devices
        row_ids = device * here + jnp.arange(here, dtype=jnp.int32)[:, None]
        away = colidx - row_ids
        away = jnp.where(away > H, away - total, jnp.where(away < -H, away + total, away))
        meta = jnp.pad(away.astype(jnp.bfloat16), ((0, META_ROWS - here), (0, LANES - slots)))
        own = jnp.concatenate([blocks.reshape(here * slots * size, size), meta], axis=0)

        def send(x, pairs):
            return lax.ppermute(x, ALL, pairs)

        down, up, swap = chip_pairs(devices, -1), chip_pairs(devices, 1), core_pairs(devices)
        s1 = send(own, down)
        s2 = send(own, up)
        f1 = send(s1, down)
        f2 = send(s2, up)
        i0 = send(own, swap)
        i1 = send(s1, swap)
        i2 = send(s2, swap)
        i3 = send(f1, swap)

        lane = jnp.arange(LANES, dtype=jnp.int32)
        row_counts = jnp.where(lane == col, counts[0, 0], 0)
        row_counts = lax.psum(row_counts, ("y", "core"))
        row_counts = lax.psum(row_counts, "x")
        within = jnp.sum(jnp.where(lane < col, row_counts, 0))
        row_total = jnp.broadcast_to(jnp.sum(row_counts), (LANES,))
        far = send(row_total, far_pairs(rows_of, cols_of))
        before = jnp.where((col >= 1) & (col <= grid_row), far, 0)
        before = lax.psum(before, ("y", "core"))
        before = lax.psum(before, "x")
        offsets = (before[0] + within).astype(jnp.int32).reshape(1, 1)

        side = 1 - 2 * (col % 2)
        tiles = here * (4 * H + 1)
        reach = jnp.arange(2 * H + 2, dtype=jnp.int32)
        spot = away + H + jnp.arange(here, dtype=jnp.int32)[:, None]
        hit = spot[:, :, None] == reach[None, None, :]
        slot = jnp.sum(jnp.where(hit, jnp.arange(1, slots + 1, dtype=jnp.int32)[None, :, None], 0), axis=1) - 1
        params = jnp.concatenate(
            [side.reshape(1), counts.reshape(1), slot.reshape(-1), out_list.reshape(-1)]
        ).astype(jnp.int32)
        by_name = {OWN: own, I0: i0, S1: s1, S2: s2, I1: i1, I2: i2, F1: f1, I3: i3, F2: f2}
        packed = products(params, [by_name[p] for p in range(9)], tiles, size, slots)
        return (packed, offsets)

    return compute


def solution(mesh):
    rows_of, cols_of = mesh.shape["row"], mesh.shape["col"]
    fine = Mesh(mesh.devices.reshape(rows_of, cols_of // 8, 4, 2), ALL)
    col = ("x", "y", "core")
    in_specs = (
        P(ALL, None, None, None),
        P(ALL, None),
        P("row", col),
        P("row", col, None),
    )
    out_specs = (P(ALL, None, None), P("row", col))
    return jax.shard_map(
        make_shards(dict(fine.shape)), mesh=fine, in_specs=in_specs, out_specs=out_specs, check_vma=False
    )
```
